128 devices in a mesh: row: 8 (over y, x_hi), col: 16 (over z, x_lo, core).
Axes of the slice: x: 4 (x_hi: 2, x_lo: 2; x = x_hi * 2 + x_lo), y: 4, z: 4, core: 2. Of those that a mesh axis runs over, the one named last changes fastest.
Arguments:
- scen_inverse: bfloat16 [256, 512, 512], P(('row', 'col')), may hold values from -32 to 32, as said below
- coupling: bfloat16 [256, 512, 3072], P(('row', 'col')), may hold values from -0.0625 to 0.0625
- scen_cot: bfloat16 [256, 512, 256], P(('row', 'col')), may hold values from -6 to 6
- first_cot: float32 [3072, 256], P('row'), may hold values from -6 to 6
- schur_inverse: float32 [3072, 3072], P('row', 'col'), may hold values from -32 to 32, as said below
- scen_primal: bfloat16 [256, 512, 256], P(('row', 'col')), may hold values from -0.375 to 0.375
- first_primal: bfloat16 [3072, 256], replicated, may hold values from -0.375 to 0.375
Outputs:
- scen_adjoint: float32 [256, 512, 256], P(('row', 'col'))
- first_adjoint: float32 [3072, 256], P('col')
- coupling_grad: float32 [256, 512, 3072], P(('row', 'col'))
The draws below stay inside these ranges and needn't reach their ends.
Inputs may be any that keep to these rules, and one draw needn't show every extreme that they name: `scen_inverse`: each block is full rank and well conditioned. `schur_inverse`: full rank and well conditioned.
All inputs are finite; a program needn't handle non-finite values.
Results may differ from the reference program's by a relative error of at most 0.005.
Values may be sent and summed in bfloat16 or wider, within the bound.
A program may use at most 128 MiB of HBM per device.

```python
import jax
import jax.numpy as jnp
from jax import lax

M = 512
N = 3072
R = 256
SCEN = 256


def dominant(key, count, order):
    first, second = jax.random.split(key, 2)
    spread = jax.random.truncated_normal(first, -4.0, 4.0, (count, order, order), jnp.float32) * (0.5 / order ** 0.5)
    middle = jax.random.uniform(second, (count, order), jnp.float32, 0.5, 1.5)
    matrix = spread + middle[:, :, None] * jnp.eye(order, dtype=jnp.float32)[None]
    return matrix


def draw_scen_inverse(key, part):
    return dominant(jax.random.fold_in(key, 11), SCEN, M).astype(jnp.bfloat16)


def draw_schur_inverse(key, part):
    return dominant(jax.random.fold_in(key, 23), 1, N)[0]


def raised(result, stream_key, source, target, shards_of, factor):
    def block_of(dim):
        return (jnp.arange(result.shape[dim]) // (result.shape[dim] // shards_of)).reshape((-1,) + (1,) * (result.ndim - 1 - dim))

    first = jax.random.permutation(stream_key, shards_of)[block_of(target)]
    other_side = (block_of(target) + shards_of // 2) % shards_of
    return jnp.where((block_of(source) == first) | (block_of(source) == other_side), factor * result, result)


def levels(own_key, dims, pieces, least, top_value):
    factor_of, own = 1.0, jax.random.fold_in(own_key, 6)
    for axis_at, parts in pieces:
        draws = jnp.exp(jax.random.uniform(jax.random.fold_in(own, axis_at), (parts,), jnp.float32, least / len(pieces), top_value / len(pieces)))
        factor_of = factor_of * jnp.repeat(draws, dims[axis_at] // parts).reshape([-1 if axis == axis_at else 1 for axis in range(len(dims))])
    return factor_of


def bell_draw(rng, extent, deviation, reach, cuts=(), kind=jnp.bfloat16):
    entries = deviation * jax.random.normal(rng, extent, jnp.float32)
    if cuts:
        entries = entries * levels(rng, extent, cuts, -0.22, 0.18)
    return jnp.clip(entries, -reach, reach).astype(kind)


def noise_with(key, shape, deviation, bound, shards, heavy, kind=jnp.bfloat16):
    array = deviation * jax.random.normal(key, shape, jnp.float32)
    if shards:
        array = array * levels(key, shape, shards, -0.22, 0.18)
    return jnp.clip(raised(array, jax.random.fold_in(key, 3), *heavy), -bound, bound).astype(kind)


def setup_inputs(seed: int = 0) -> dict:
    splits = jax.random.split(jax.random.key(seed), 8)
    return {
        "scen_inverse": draw_scen_inverse(jax.random.fold_in(splits[7], 71), 0),
        "coupling": noise_with(splits[1], (SCEN, M, N), (SCEN * M) ** -0.5, 0.0625, ((0, 128),), (0, 2, 128, 5.5)),
        "scen_cot": bell_draw(splits[2], (SCEN, M, R), 1.0, 6.0, ((0, 128),)),
        "first_cot": bell_draw(splits[3], (N, R), 1.0, 6.0, ((0, 8),), jnp.float32),
        "schur_inverse": draw_schur_inverse(jax.random.fold_in(splits[7], 71), 0),
        "scen_primal": bell_draw(splits[5], (SCEN, M, R), R ** -0.5, 0.375, ((0, 128),)),
        "first_primal": bell_draw(splits[6], (N, R), R ** -0.5, 0.375),
    }


def reference(scen_inverse, coupling, scen_cot, first_cot, schur_inverse, scen_primal, first_primal):
    def condense(total, item):
        inverse, couple, cot = item
        helper = jnp.dot(inverse.T, cot, preferred_element_type=jnp.float32).astype(jnp.bfloat16)
        return total + jnp.dot(couple.T, helper, preferred_element_type=jnp.float32), None

    summed, _ = lax.scan(condense, jnp.zeros((N, R), jnp.float32), (scen_inverse, coupling, scen_cot))
    condensed = first_cot - summed
    first_adjoint = jnp.dot(schur_inverse.T, condensed, precision=lax.Precision.HIGHEST, preferred_element_type=jnp.float32)
    adjoint_low = first_adjoint.astype(jnp.bfloat16)

    def recover(item):
        inverse, couple, cot, primal = item
        update = (cot.astype(jnp.float32) - jnp.dot(couple, adjoint_low, preferred_element_type=jnp.float32)).astype(jnp.bfloat16)
        adjoint = jnp.dot(inverse.T, update, preferred_element_type=jnp.float32)
        scen_low = adjoint.astype(jnp.bfloat16)
        gradient = -(jnp.dot(scen_low, first_primal.T, preferred_element_type=jnp.float32) + jnp.dot(primal, adjoint_low.T, preferred_element_type=jnp.float32))
        return adjoint, gradient

    scen_adjoint, coupling_grad = lax.map(recover, (scen_inverse, coupling, scen_cot, scen_primal))
    return scen_adjoint, first_adjoint, coupling_grad
```

```python
import functools

import jax
import jax.numpy as jnp
from jax import lax
from jax.experimental import pallas as pl
from jax.experimental.pallas import tpu as pltpu
from jax.sharding import PartitionSpec as P

MESH = pl.DeviceIdType.MESH
F32, BF16 = jnp.float32, jnp.bfloat16
FAR_FIRST = (2, 1, 3, 0)
NT = (((1,), (1,)), ((), ()))
TN = (((0,), (0,)), ((), ()))


def place():
    row, col = lax.axis_index("row"), lax.axis_index("col")
    return (row % 2) * 2 + (col // 2) % 2, row // 2, col // 4, col % 2


def device(x, y, z, core):
    return (y * 2 + x // 2, z * 4 + (x % 2) * 2 + core)


def part(start, size):
    return pl.ds(pl.multiple_of(start, size), size)


def wait_for(ref, sem):
    pltpu.make_async_copy(ref, ref, sem).wait()


def exchange(
    inverse_hbm, coupling_hbm, cot_hbm, first_hbm, schur_hbm,
    adjoint_hbm, q_ref,
    inverse, coupling, cot, first, schur, first_t, h_t, split,
    pair_send, pair_own, pair_recv, ring_send, ring_recv, plane_send, plane_recv,
    condensed, product, product_recv, adjoint,
    load_sem, chunk_sem, pair_ssem, pair_rsem, schur_ssem, schur_rsem, ring_ssem, ring_rsem,
    plane_ssem, plane_rsem, gather_ssem, gather_rsem, product_ssem, product_rsem,
    spread_ssem, spread_rsem, forward_ssem, forward_rsem, out_sem,
):
    x, y, z, core = place()
    x_hi, x_lo = x // 2, x % 2
    block, tile = y * 2 + x_hi, z * 2 + x_lo
    partner = device(x, y, z, 1 - core)

    def send(source, target, ssem, rsem, to):
        copy = pltpu.make_async_remote_copy(
            src_ref=source, dst_ref=target, send_sem=ssem, recv_sem=rsem, device_id=to, device_id_type=MESH
        )
        copy.start()

    barrier = pltpu.get_barrier_semaphore()
    for dx in range(4):
        for dy in range(4):
            for dz in range(4):
                if (dx, dy, dz) != (0, 0, 0):
                    there = device((x + dx) % 4, (y + dy) % 4, (z + dz) % 4, core)
                    pl.semaphore_signal(barrier, inc=1, device_id=there, device_id_type=MESH)
    pl.semaphore_signal(barrier, inc=1, device_id=partner, device_id_type=MESH)

    loads = [
        pltpu.make_async_copy(cot_hbm, cot, load_sem.at[0]),
        pltpu.make_async_copy(inverse_hbm, inverse, load_sem.at[1]),
    ]
    for copy in loads:
        copy.start()
    chunks = []
    for k, dy in enumerate(FAR_FIRST):
        lanes = part(((y + dy) % 4) * 768, 768)
        chunks.append(
            pltpu.make_async_copy(coupling_hbm.at[:, :, lanes], coupling.at[:, :, lanes], chunk_sem.at[k])
        )
        chunks[-1].start()
    late = [
        pltpu.make_async_copy(first_hbm, first, load_sem.at[2]),
        pltpu.make_async_copy(schur_hbm, schur.at[core], load_sem.at[3]),
    ]
    for copy in late:
        copy.start()

    for copy in loads:
        copy.wait()
    for s in range(2):
        helper = lax.dot_general(cot[s], inverse[s], TN, preferred_element_type=F32).astype(BF16)
        h_t[part((1 - core) * 128, 128), s * 512 : (s + 1) * 512] = helper[:128]
        h_t[part(core * 128, 128), s * 512 : (s + 1) * 512] = helper[128:]

    pl.semaphore_wait(barrier, 64)
    for copy in late:
        copy.wait()
    send(schur.at[core], schur.at[core], schur_ssem, schur_rsem, partner)

    def local_sum(k):
        lanes = part(((y + FAR_FIRST[k]) % 4) * 768, 768)
        chunks[k].wait()
        total = jnp.dot(h_t[:, :512], coupling[0, :, lanes], preferred_element_type=F32)
        total += jnp.dot(h_t[:, 512:], coupling[1, :, lanes], preferred_element_type=F32)
        pair_send[k] = total[:128].astype(BF16)
        pair_own[k] = total[128:]
        send(pair_send.at[k], pair_recv.at[k], pair_ssem, pair_rsem.at[k], partner)

    def to_ring(k):
        wait_for(pair_recv.at[k], pair_rsem.at[k])
        ring_send[k] = (pair_own[k] + pair_recv[k].astype(F32)).astype(BF16)
        for dx in (2, 1, 3):
            there = (x + dx) % 4
            send(
                ring_send.at[k, part((there % 2) * 64, 64), part((there // 2) * 384, 384)],
                ring_recv.at[dx - 1, k],
                ring_ssem,
                ring_rsem.at[dx - 1, k],
                device(there, y, z, core),
            )

    local_sum(0)
    for k in range(1, 4):
        local_sum(k)
        to_ring(k - 1)
    to_ring(3)

    first_t[...] = first[:, part(core * 128, 128)].T
    wait_for(schur.at[1 - core], schur_rsem)
    whole = schur[...].reshape(384, 384)
    high = whole.astype(BF16)
    split[0] = high
    split[1] = (whole - high.astype(F32)).astype(BF16)

    for k in range(4):
        total = ring_send[k, part(x_lo * 64, 64), part(x_hi * 384, 384)].astype(F32)
        for d in range(3):
            wait_for(ring_recv.at[d, k], ring_rsem.at[d, k])
            total += ring_recv[d, k].astype(F32)
        plane_send[k] = total.astype(BF16)
        for j, dz in enumerate(FAR_FIRST):
            if (k, j) != (3, 3):
                there = (z + dz) % 4
                send(
                    plane_send.at[k, part(there * 16, 16)],
                    plane_recv.at[k * 4 + j],
                    plane_ssem,
                    plane_rsem,
                    device(x, (y + FAR_FIRST[k]) % 4, there, core),
                )

    total = plane_send[3, part(z * 16, 16)].astype(F32)
    wait_for(plane_recv, plane_rsem)
    for k in range(15):
        total += plane_recv[k].astype(F32)
    slot = x_lo * 4 + z
    condensed[slot] = first_t[part(slot * 16, 16)] - total
    for dx in range(2):
        for dz in FAR_FIRST:
            if (dx, dz) != (0, 0):
                there = device(x_hi * 2 + (x_lo + dx) % 2, y, (z + dz) % 4, core)
                send(condensed.at[slot], condensed.at[slot], gather_ssem, gather_rsem, there)
    wait_for(condensed.at[pl.ds(0, 7)], gather_rsem)

    rows = condensed[...].reshape(128, 384)
    high = rows.astype(BF16)
    low = (rows - high.astype(F32)).astype(BF16)
    result = lax.dot_general(high, split[0], NT, preferred_element_type=F32)
    result += lax.dot_general(high, split[1], NT, preferred_element_type=F32)
    result += lax.dot_general(low, split[0], NT, preferred_element_type=F32)
    product[...] = result.reshape(8, 16, 384)
    for dy in FAR_FIRST:
        for dx in range(2):
            if (dx, dy) != (0, 0):
                there_y, there_x = (y + dy) % 4, (x_hi + dx) % 2
                send(
                    product.at[there_y * 2 + there_x],
                    product_recv.at[dy * 2 + dx - 1],
                    product_ssem,
                    product_rsem,
                    device(there_x * 2 + x_lo, there_y, z, core),
                )
    total = product[block]
    wait_for(product_recv, product_rsem)
    for k in range(7):
        total += product_recv[k]

    def spot(x, y, z):
        return adjoint.at[part(core * 128 + (y * 2 + x // 2) * 16, 16), part((z * 2 + x % 2) * 384, 384)]

    mine = spot(x, y, z)
    mine[...] = total.astype(BF16)
    send(mine, mine, forward_ssem, forward_rsem, partner)
    shifts = [(dx, dy, dz) for dx in FAR_FIRST for dy in FAR_FIRST for dz in FAR_FIRST][:63]
    for n, (dx, dy, dz) in enumerate(shifts):
        there = device((x + dx) % 4, (y + dy) % 4, (z + dz) % 4, core)
        send(mine, mine, spread_ssem.at[n], spread_rsem.at[n], there)
    for n, (dx, dy, dz) in enumerate(shifts):
        got = spot((x - dx) % 4, (y - dy) % 4, (z - dz) % 4)
        wait_for(got, spread_rsem.at[n])
        send(got, got, forward_ssem, forward_rsem, partner)
    wait_for(adjoint.at[part((1 - core) * 128, 128)], forward_rsem)
    out = pltpu.make_async_copy(adjoint, adjoint_hbm, out_sem)
    out.start()
    for s in range(2):
        took = lax.dot_general(coupling[s], adjoint[...], NT, preferred_element_type=F32)
        q_ref[s] = (cot[s].astype(F32) - took).astype(BF16)
    out.wait()

    wait_for(schur.at[core], schur_ssem)
    wait_for(pair_send, pair_ssem)
    wait_for(ring_recv, ring_ssem)
    wait_for(plane_recv, plane_ssem)
    wait_for(condensed.at[pl.ds(0, 7)], gather_ssem)
    wait_for(product_recv, product_ssem)
    for n in range(63):
        wait_for(mine, spread_ssem.at[n])
    wait_for(adjoint.at[part(core * 128, 128)], forward_ssem)


def gradients(inverse, q, primal, first_primal, adjoint, columns, scen_ref, first_ref, grad_ref, left):
    @pl.when(pl.program_id(0) == 0)
    def _():
        for s in range(2):
            value = lax.dot_general(inverse[s], q[s], TN, preferred_element_type=F32)
            scen_ref[s] = value
            left[s, :, :256] = -value.astype(BF16)
            left[s, :, 256:] = -primal[s]
        first_ref[...] = columns[...].astype(F32).T

    for s in range(2):
        grad = lax.dot_general(left[s, :, :256], first_primal[...], NT, preferred_element_type=F32)
        grad_ref[s] = grad + jnp.dot(left[s, :, 256:], adjoint[...], preferred_element_type=F32)


def body(scen_inverse, coupling, scen_cot, first_cot, schur_inverse, scen_primal, first_primal):
    any_space = pl.BlockSpec(memory_space=pl.ANY)
    dma = pltpu.SemaphoreType.DMA
    adjoint, q = pl.pallas_call(
        exchange,
        out_shape=(jax.ShapeDtypeStruct((256, 3072), BF16), jax.ShapeDtypeStruct((2, 512, 256), BF16)),
        in_specs=[any_space] * 5,
        out_specs=(any_space, pl.BlockSpec(memory_space=pltpu.VMEM)),
        scratch_shapes=[
            pltpu.VMEM((2, 512, 512), BF16),
            pltpu.VMEM((2, 512, 3072), BF16),
            pltpu.VMEM((2, 512, 256), BF16),
            pltpu.VMEM((384, 256), F32),
            pltpu.VMEM((2, 192, 384), F32),
            pltpu.VMEM((128, 384), F32),
            pltpu.VMEM((256, 1024), BF16),
            pltpu.VMEM((2, 384, 384), BF16),
            pltpu.VMEM((4, 128, 768), BF16),
            pltpu.VMEM((4, 128, 768), F32),
            pltpu.VMEM((4, 128, 768), BF16),
            pltpu.VMEM((4, 128, 768), BF16),
            pltpu.VMEM((3, 4, 64, 384), BF16),
            pltpu.VMEM((4, 64, 384), BF16),
            pltpu.VMEM((15, 16, 384), BF16),
            pltpu.VMEM((8, 16, 384), F32),
            pltpu.VMEM((8, 16, 384), F32),
            pltpu.VMEM((7, 16, 384), F32),
            pltpu.VMEM((256, 3072), BF16),
            dma((4,)), dma((4,)), dma, dma((4,)), dma, dma, dma, dma((3, 4)),
            dma, dma, dma, dma, dma, dma,
            dma((63,)), dma((63,)), dma, dma, dma,
        ],
        compiler_params=pltpu.CompilerParams(
            collective_id=0, has_side_effects=True, vmem_limit_bytes=40 * 1024 * 1024
        ),
        name="exchange",
    )(scen_inverse, coupling, scen_cot, first_cot, schur_inverse.T)
    column = lax.axis_index("col")
    columns = lax.dynamic_slice(adjoint, (0, column * 192), (256, 192))
    step = 256
    whole = lambda *shape: pl.BlockSpec(shape, lambda n: (0,) * len(shape), pipeline_mode=pl.Buffered(1))
    scen_adjoint, first_adjoint, coupling_grad = pl.pallas_call(
        gradients,
        out_shape=(
            jax.ShapeDtypeStruct((2, 512, 256), F32),
            jax.ShapeDtypeStruct((192, 256), F32),
            jax.ShapeDtypeStruct((2, 512, 3072), F32),
        ),
        grid=(3072 // step,),
        in_specs=[
            whole(2, 512, 512),
            whole(2, 512, 256),
            whole(2, 512, 256),
            pl.BlockSpec((step, 256), lambda n: (n, 0)),
            pl.BlockSpec((256, step), lambda n: (0, n)),
            whole(256, 192),
        ],
        out_specs=(
            whole(2, 512, 256),
            whole(192, 256),
            pl.BlockSpec((2, 512, step), lambda n: (0, 0, n)),
        ),
        scratch_shapes=[pltpu.VMEM((2, 512, 512), BF16)],
        compiler_params=pltpu.CompilerParams(vmem_limit_bytes=40 * 1024 * 1024),
        name="gradients",
    )(scen_inverse, q, scen_primal, first_primal, adjoint, columns)
    return scen_adjoint, first_adjoint, coupling_grad


def solution(mesh):
    return jax.shard_map(
        body,
        mesh=mesh,
        in_specs=(
            P(("row", "col"), None, None),
            P(("row", "col"), None, None),
            P(("row", "col"), None, None),
            P("row", None),
            P("row", "col"),
            P(("row", "col"), None, None),
            P(),
        ),
        out_specs=(P(("row", "col"), None, None), P("col", None), P(("row", "col"), None, None)),
        check_vma=False,
    )
```

```python
import functools

import jax
import jax.numpy as jnp
from jax import lax
from jax.experimental import pallas as pl
from jax.experimental.pallas import tpu as pltpu
from jax.sharding import PartitionSpec as P

MESH = pl.DeviceIdType.MESH
F32, BF16 = jnp.float32, jnp.bfloat16
FAR_FIRST = (2, 1, 3, 0)
NT = (((1,), (1,)), ((), ()))
TN = (((0,), (0,)), ((), ()))


def place():
    row, col = lax.axis_index("row"), lax.axis_index("col")
    return (row % 2) * 2 + (col // 2) % 2, row // 2, col // 4, col % 2


def device(x, y, z, core):
    return (y * 2 + x // 2, z * 4 + (x % 2) * 2 + core)


def part(start, size):
    return pl.ds(pl.multiple_of(start, size), size)


def wait_for(ref, sem):
    pltpu.make_async_copy(ref, ref, sem).wait()


def exchange(
    inverse_hbm, coupling_hbm, cot_hbm, first_hbm, schur_hbm, primal_hbm,
    adjoint_hbm, scen_ref, left_ref,
    inverse, inverse_t, coupling, cot, primal, first, schur, first_t, h_t, split,
    pair_send, pair_own, pair_recv, ring_send, ring_recv, plane_send, plane_recv,
    condensed, product, product_recv, adjoint, taken,
    load_sem, chunk_sem, near_sem, pair_ssem, pair_rsem, schur_ssem, schur_rsem, ring_ssem, ring_rsem,
    plane_ssem, plane_rsem, gather_ssem, gather_rsem, product_ssem, product_rsem,
    spread_ssem, spread_rsem, forward_ssem, forward_rsem, out_sem,
):
    x, y, z, core = place()
    x_hi, x_lo = x // 2, x % 2
    block, tile = y * 2 + x_hi, z * 2 + x_lo
    partner = device(x, y, z, 1 - core)
    drains = []

    def finish():
        for ref, sem in drains:
            wait_for(ref, sem)

    def send(source, target, ssem, rsem, to):
        copy = pltpu.make_async_remote_copy(
            src_ref=source, dst_ref=target, send_sem=ssem, recv_sem=rsem, device_id=to, device_id_type=MESH
        )
        copy.start()

    barrier = pltpu.get_barrier_semaphore()
    rings = [device((x + d) % 4, y, z, core) for d in (1, 2, 3)]
    y_ring = [device(x, (y + d) % 4, z, core) for d in (1, 2, 3)]
    rings += y_ring + [device(x, y, (z + d) % 4, core) for d in (1, 2, 3)]
    for there in rings + [partner]:
        pl.semaphore_signal(barrier, inc=1, device_id=there, device_id_type=MESH)

    loads = [
        pltpu.make_async_copy(cot_hbm, cot, load_sem.at[0]),
        pltpu.make_async_copy(inverse_hbm, inverse, load_sem.at[1]),
    ]
    for copy in loads:
        copy.start()
    chunks = []
    for k, dy in enumerate(FAR_FIRST):
        lanes = part(((y + dy) % 4) * 768, 768)
        chunks.append(
            pltpu.make_async_copy(coupling_hbm.at[:, :, lanes], coupling.at[:, :, lanes], chunk_sem.at[k])
        )
        chunks[-1].start()
    late = [
        pltpu.make_async_copy(first_hbm, first, load_sem.at[2]),
        pltpu.make_async_copy(schur_hbm, schur.at[core], load_sem.at[3]),
        pltpu.make_async_copy(primal_hbm, primal, load_sem.at[4]),
    ]
    for copy in late:
        copy.start()

    for copy in loads:
        copy.wait()
    for s in range(2):
        helper = lax.dot_general(cot[s], inverse[s], TN, preferred_element_type=F32).astype(BF16)
        h_t[part((1 - core) * 128, 128), s * 512 : (s + 1) * 512] = helper[:128]
        h_t[part(core * 128, 128), s * 512 : (s + 1) * 512] = helper[128:]

    def local_sum(k):
        lanes = part(((y + FAR_FIRST[k]) % 4) * 768, 768)
        chunks[k].wait()
        total = jnp.dot(h_t[:, :512], coupling[0, :, lanes], preferred_element_type=F32)
        total += jnp.dot(h_t[:, 512:], coupling[1, :, lanes], preferred_element_type=F32)
        pair_send[k] = total[:128].astype(BF16)
        pair_own[k] = total[128:]

    def to_pair(k):
        send(pair_send.at[k], pair_recv.at[k], pair_ssem, pair_rsem.at[k], partner)

    def to_ring(k):
        wait_for(pair_recv.at[k], pair_rsem.at[k])
        ring_send[k] = (pair_own[k] + pair_recv[k].astype(F32)).astype(BF16)
        for dx in (2, 1, 3):
            there = (x + dx) % 4
            send(
                ring_send.at[k, part((there % 2) * 64, 64), part((there // 2) * 384, 384)],
                ring_recv.at[dx - 1, k],
                ring_ssem,
                ring_rsem.at[dx - 1, k],
                device(there, y, z, core),
            )

    drains.append((pair_send, pair_ssem))
    drains.append((ring_recv, ring_ssem))
    local_sum(0)
    pl.semaphore_wait(barrier, 10)
    to_pair(0)
    for there in y_ring:
        pl.semaphore_signal(near_sem, inc=1, device_id=there, device_id_type=MESH)
    for k in range(1, 4):
        local_sum(k)
        to_pair(k)
        to_ring(k - 1)
    for copy in late:
        copy.wait()
    send(schur.at[core], schur.at[core], schur_ssem, schur_rsem, partner)
    drains.append((schur.at[core], schur_ssem))
    to_ring(3)

    pl.semaphore_wait(near_sem, 3)
    drains.append((plane_recv, plane_ssem))
    for k in range(4):
        total = ring_send[k, part(x_lo * 64, 64), part(x_hi * 384, 384)].astype(F32)
        for d in range(3):
            wait_for(ring_recv.at[d, k], ring_rsem.at[d, k])
            total += ring_recv[d, k].astype(F32)
        plane_send[k] = total.astype(BF16)
        for j, dz in enumerate(FAR_FIRST):
            if (k, j) != (3, 3):
                there = (z + dz) % 4
                send(
                    plane_send.at[k, part(there * 16, 16)],
                    plane_recv.at[k * 4 + j],
                    plane_ssem,
                    plane_rsem,
                    device(x, (y + FAR_FIRST[k]) % 4, there, core),
                )

    first_t[...] = first[:, part(core * 128, 128)].T
    wait_for(schur.at[1 - core], schur_rsem)
    whole = schur[...].reshape(384, 384)
    high = whole.astype(BF16)
    split[0] = high
    split[1] = (whole - high.astype(F32)).astype(BF16)
    total = plane_send[3, part(z * 16, 16)].astype(F32)
    wait_for(plane_recv, plane_rsem)
    for k in range(15):
        total += plane_recv[k].astype(F32)
    slot = x_lo * 4 + z
    condensed[slot] = first_t[part(slot * 16, 16)] - total
    drains.append((condensed.at[pl.ds(0, 7)], gather_ssem))
    for dx in (1, 0):
        for dz in FAR_FIRST:
            if (dx, dz) != (0, 0):
                there = device(x_hi * 2 + (x_lo + dx) % 2, y, (z + dz) % 4, core)
                send(condensed.at[slot], condensed.at[slot], gather_ssem, gather_rsem, there)
    inverse_t[0] = inverse[0].T
    inverse_t[1] = inverse[1].T
    wait_for(condensed.at[pl.ds(0, 7)], gather_rsem)

    rows = condensed[...].reshape(128, 384)
    high = rows.astype(BF16)
    low = (rows - high.astype(F32)).astype(BF16)
    result = lax.dot_general(high, split[0], NT, preferred_element_type=F32)
    result += lax.dot_general(high, split[1], NT, preferred_element_type=F32)
    result += lax.dot_general(low, split[0], NT, preferred_element_type=F32)
    product[...] = result.reshape(8, 16, 384)
    drains.append((product_recv, product_ssem))
    for dx in (1, 0):
        for dy in FAR_FIRST:
            if (dx, dy) != (0, 0):
                there_y, there_x = (y + dy) % 4, (x_hi + dx) % 2
                send(
                    product.at[there_y * 2 + there_x],
                    product_recv.at[dy * 2 + dx - 1],
                    product_ssem,
                    product_rsem,
                    device(there_x * 2 + x_lo, there_y, z, core),
                )
    for s in range(2):
        left_ref[s, :, 256:] = -primal[s]
    total = product[block]
    wait_for(product_recv, product_rsem)
    for k in range(7):
        total += product_recv[k]

    def spot(x, y, z):
        return adjoint.at[part(core * 128 + (y * 2 + x // 2) * 16, 16), part((z * 2 + x % 2) * 384, 384)]

    mine = spot(x, y, z)
    mine[...] = total.astype(BF16)
    shifts = [(dx, dy, dz) for dz in FAR_FIRST for dx in FAR_FIRST for dy in FAR_FIRST][:63]
    for n, (dx, dy, dz) in enumerate(shifts):
        there = device((x + dx) % 4, (y + dy) % 4, (z + dz) % 4, core)
        send(mine, mine, spread_ssem.at[n], spread_rsem.at[n], there)
        drains.append((mine, spread_ssem.at[n]))
    send(mine, mine, forward_ssem, forward_rsem.at[3], partner)

    def take(group):
        lanes = part(((z - FAR_FIRST[group]) % 4) * 768, 768)
        theirs = adjoint.at[part((1 - core) * 128, 128), lanes]
        wait_for(theirs, forward_rsem.at[group])
        for s in range(2):
            term = lax.dot_general(coupling[s, :, lanes], adjoint[:, lanes], NT, preferred_element_type=F32)
            if group == 0:
                taken[s] = term
            else:
                taken[s] += term

    for group in range(4):
        for n in range(group * 16, min(group * 16 + 16, 63)):
            dx, dy, dz = shifts[n]
            got = spot((x - dx) % 4, (y - dy) % 4, (z - dz) % 4)
            wait_for(got, spread_rsem.at[n])
            send(got, got, forward_ssem, forward_rsem.at[group], partner)
        if group:
            take(group - 1)
    drains.append((adjoint.at[part(core * 128, 128)], forward_ssem))
    wait_for(adjoint.at[part((1 - core) * 128, 128), part(z * 768, 768)], forward_rsem.at[3])
    out = pltpu.make_async_copy(adjoint, adjoint_hbm, out_sem)
    out.start()
    lanes = part(z * 768, 768)
    for s in range(2):
        term = lax.dot_general(coupling[s, :, lanes], adjoint[:, lanes], NT, preferred_element_type=F32)
        q = (cot[s].astype(F32) - (taken[s] + term)).astype(BF16)
        value = jnp.dot(inverse_t[s], q, preferred_element_type=F32)
        scen_ref[s] = value
        left_ref[s, :, :256] = -value.astype(BF16)
    out.wait()
    finish()


STEP = 256


def gradients(left, first_primal, adjoint, scen, columns, scen_hbm, first_ref, grad_hbm, buffer, scen_sem, sems):
    scen_copy = pltpu.make_async_copy(scen, scen_hbm, scen_sem)
    scen_copy.start()

    def write(n):
        return pltpu.make_async_copy(
            buffer.at[n % 3], grad_hbm.at[:, :, part(n * STEP, STEP)], sems.at[n % 3]
        )

    def step(n, carry):
        @pl.when(n >= 3)
        def _():
            write(n - 3).wait()

        at = part(n * STEP, STEP)
        for s in range(2):
            grad = lax.dot_general(left[s, :, :256], first_primal[at], NT, preferred_element_type=F32)
            buffer[n % 3, s] = grad + jnp.dot(left[s, :, 256:], adjoint[:, at], preferred_element_type=F32)
        write(n).start()
        return carry

    steps = 3072 // STEP
    lax.fori_loop(0, steps, step, 0)
    first_ref[...] = columns[...].astype(F32).T
    for n in range(steps - 3, steps):
        write(n).wait()
    scen_copy.wait()


def body(scen_inverse, coupling, scen_cot, first_cot, schur_inverse, scen_primal, first_primal):
    any_space, vmem = pl.BlockSpec(memory_space=pl.ANY), pl.BlockSpec(memory_space=pltpu.VMEM)
    dma = pltpu.SemaphoreType.DMA
    operands = (scen_inverse, coupling, scen_cot, first_cot, schur_inverse.T, scen_primal)
    adjoint, scen, left = pl.pallas_call(
        exchange,
        out_shape=(
            jax.ShapeDtypeStruct((256, 3072), BF16),
            jax.ShapeDtypeStruct((2, 512, 256), F32),
            jax.ShapeDtypeStruct((2, 512, 512), BF16),
        ),
        in_specs=[any_space] * 6,
        out_specs=(any_space, vmem, vmem),
        scratch_shapes=[
            pltpu.VMEM((2, 512, 512), BF16),
            pltpu.VMEM((2, 512, 512), BF16),
            pltpu.VMEM((2, 512, 3072), BF16),
            pltpu.VMEM((2, 512, 256), BF16),
            pltpu.VMEM((2, 512, 256), BF16),
            pltpu.VMEM((384, 256), F32),
            pltpu.VMEM((2, 192, 384), F32),
            pltpu.VMEM((128, 384), F32),
            pltpu.VMEM((256, 1024), BF16),
            pltpu.VMEM((2, 384, 384), BF16),
            pltpu.VMEM((4, 128, 768), BF16),
            pltpu.VMEM((4, 128, 768), F32),
            pltpu.VMEM((4, 128, 768), BF16),
            pltpu.VMEM((4, 128, 768), BF16),
            pltpu.VMEM((3, 4, 64, 384), BF16),
            pltpu.VMEM((4, 64, 384), BF16),
            pltpu.VMEM((15, 16, 384), BF16),
            pltpu.VMEM((8, 16, 384), F32),
            pltpu.VMEM((8, 16, 384), F32),
            pltpu.VMEM((7, 16, 384), F32),
            pltpu.VMEM((256, 3072), BF16),
            pltpu.VMEM((2, 512, 256), F32),
            dma((5,)), dma((4,)), pltpu.SemaphoreType.REGULAR, dma, dma((4,)), dma, dma, dma, dma((3, 4)),
            dma, dma, dma, dma, dma, dma,
            dma((63,)), dma((63,)), dma, dma((4,)), dma,
        ],
        compiler_params=pltpu.CompilerParams(
            collective_id=0, has_side_effects=True, vmem_limit_bytes=36 * 1024 * 1024
        ),
        name="exchange",
    )(*(pltpu.with_memory_space_constraint(array, pltpu.HBM) for array in operands))
    columns = lax.dynamic_slice(adjoint, (0, lax.axis_index("col") * 192), (256, 192))
    return pl.pallas_call(
        gradients,
        out_shape=(
            jax.ShapeDtypeStruct((2, 512, 256), F32),
            jax.ShapeDtypeStruct((192, 256), F32),
            jax.ShapeDtypeStruct((2, 512, 3072), F32),
        ),
        in_specs=[vmem] * 5,
        out_specs=(any_space, vmem, any_space),
        scratch_shapes=[pltpu.VMEM((3, 2, 512, STEP), F32), dma, dma((3,))],
        compiler_params=pltpu.CompilerParams(vmem_limit_bytes=24 * 1024 * 1024),
        name="gradients",
    )(left, first_primal, adjoint, scen, columns)


def solution(mesh):
    return jax.shard_map(
        body,
        mesh=mesh,
        in_specs=(
            P(("row", "col"), None, None),
            P(("row", "col"), None, None),
            P(("row", "col"), None, None),
            P("row", None),
            P("row", "col"),
            P(("row", "col"), None, None),
            P(),
        ),
        out_specs=(P(("row", "col"), None, None), P("col", None), P(("row", "col"), None, None)),
        check_vma=False,
    )
```

```python
import functools

import jax
import jax.numpy as jnp
from jax import lax
from jax.experimental import pallas as pl
from jax.experimental.pallas import tpu as pltpu
from jax.sharding import PartitionSpec as P

MESH = pl.DeviceIdType.MESH
F32, BF16 = jnp.float32, jnp.bfloat16
FAR_FIRST = (2, 1, 3, 0)
NT = (((1,), (1,)), ((), ()))
TN = (((0,), (0,)), ((), ()))


def place():
    row, col = lax.axis_index("row"), lax.axis_index("col")
    return (row % 2) * 2 + (col // 2) % 2, row // 2, col // 4, col % 2


def device(x, y, z, core):
    return (y * 2 + x // 2, z * 4 + (x % 2) * 2 + core)


def part(start, size):
    return pl.ds(pl.multiple_of(start, size), size)


def wait_for(ref, sem):
    pltpu.make_async_copy(ref, ref, sem).wait()


def exchange(
    inverse_hbm, coupling_hbm, cot_hbm, first_hbm, schur_hbm, primal_hbm, base_hbm,
    scen_ref, left_ref, right_ref,
    inverse, inverse_t, coupling, cot, primal, base, first, schur, first_t, h_t, split,
    pair_send, pair_own, pair_recv, ring_send, ring_recv, plane_send, plane_recv,
    condensed, product, product_recv, adjoint, taken,
    load_sem, chunk_sem, pair_ssem, pair_rsem, schur_ssem, schur_rsem,
    near_sem, ring_ssem, ring_rsem, plane_ssem, plane_rsem,
    gather_ssem, gather_rsem, product_ssem, product_rsem,
    spread_ssem, spread_rsem, forward_ssem, forward_rsem, out_sem,
):
    x, y, z, core = place()
    x_hi, x_lo = x // 2, x % 2
    block, tile = y * 2 + x_hi, z * 2 + x_lo
    partner = device(x, y, z, 1 - core)
    drains = []

    def finish():
        for ref, sem in drains:
            wait_for(ref, sem)

    def send(source, target, ssem, rsem, to):
        copy = pltpu.make_async_remote_copy(
            src_ref=source, dst_ref=target, send_sem=ssem, recv_sem=rsem, device_id=to, device_id_type=MESH
        )
        copy.start()

    loads = [
        pltpu.make_async_copy(cot_hbm, cot, load_sem.at[0]),
        pltpu.make_async_copy(inverse_hbm, inverse, load_sem.at[1]),
    ]
    for copy in loads:
        copy.start()
    chunks = []
    for k, dy in enumerate(FAR_FIRST):
        lanes = part(((y + dy) % 4) * 768, 768)
        chunks.append(
            pltpu.make_async_copy(coupling_hbm.at[:, :, lanes], coupling.at[:, :, lanes], chunk_sem.at[k])
        )
    chunks[0].start()
    chunks[1].start()

    here = (x, y, z)

    def moved(*steps):
        spot = [(c + d) % 4 for c, d in zip(here, steps)]
        return device(*spot, core)

    barrier = pltpu.get_barrier_semaphore()
    x_ring = [moved(d, 0, 0) for d in (1, 2, 3)]
    y_ring = [moved(0, d, 0) for d in (1, 2, 3)]
    z_ring = [moved(0, 0, d) for d in (1, 2, 3)]
    for there in x_ring + y_ring + z_ring + [partner]:
        pl.semaphore_signal(barrier, inc=1, device_id=there, device_id_type=MESH)

    late = [
        pltpu.make_async_copy(first_hbm, first, load_sem.at[2]),
        pltpu.make_async_copy(schur_hbm, schur.at[core], load_sem.at[3]),
        pltpu.make_async_copy(primal_hbm, primal, load_sem.at[4]),
        pltpu.make_async_copy(base_hbm, base, load_sem.at[5]),
    ]
    for copy in loads:
        copy.wait()
    for copy in chunks[2:] + late:
        copy.start()
    for s in range(2):
        helper = lax.dot_general(cot[s], inverse[s], TN, preferred_element_type=F32).astype(BF16)
        h_t[part((1 - core) * 128, 128), s * 512 : (s + 1) * 512] = helper[:128]
        h_t[part(core * 128, 128), s * 512 : (s + 1) * 512] = helper[128:]

    def local_sum(k):
        lanes = part(((y + FAR_FIRST[k]) % 4) * 768, 768)
        chunks[k].wait()
        total = jnp.dot(h_t[...], coupling[:, :, lanes].reshape(1024, 768), preferred_element_type=F32)
        pair_send[k] = total[:128].astype(BF16)
        pair_own[k] = total[128:]

    def to_pair(k):
        send(pair_send.at[k], pair_recv.at[k], pair_ssem, pair_rsem.at[k], partner)

    def to_rings(k):
        wait_for(pair_recv.at[k], pair_rsem.at[k])
        there_y = (y + FAR_FIRST[k]) % 4
        total = (pair_own[k] + pair_recv[k].astype(F32)).astype(BF16)
        for hi in range(2):
            for lo in range(2):
                column = hi * 2 + lo
                for p in range(3):
                    lane = hi * 384 + p * 128
                    tiles = total[lo * 64 : lo * 64 + 64, lane : lane + 128].reshape(4, 16, 128)
                    if p == 0:
                        ring_send[0, column, there_y] = tiles
                    elif p == 1:
                        ring_send[1, there_y, column] = tiles
                    else:
                        ring_send[2, :, there_y, column] = tiles
        for d in (2, 1, 3):
            for p, own in ((0, x), (2, z)):
                send(
                    ring_send.at[p, (own + d) % 4, there_y],
                    ring_recv.at[p, d - 1, there_y],
                    ring_ssem.at[p],
                    ring_rsem.at[p, d - 1],
                    (x_ring if p == 0 else z_ring)[d - 1],
                )
        d = FAR_FIRST[k]
        if d:
            send(ring_send.at[1, there_y], ring_recv.at[1, d - 1], ring_ssem.at[1], ring_rsem.at[1, d - 1], y_ring[d - 1])

    drains.append((pair_send, pair_ssem))
    for p in range(3):
        drains.append((ring_recv.at[p], ring_ssem.at[p]))
    local_sum(0)
    pl.semaphore_wait(barrier, 10)
    to_pair(0)
    for there in x_ring + y_ring:
        pl.semaphore_signal(near_sem, inc=1, device_id=there, device_id_type=MESH)
    local_sum(1)
    to_pair(1)
    to_rings(0)
    local_sum(2)
    to_pair(2)
    to_rings(1)
    local_sum(3)
    to_pair(3)
    to_rings(2)
    to_rings(3)

    pl.semaphore_wait(near_sem, 6)
    drains.append((plane_recv.at[:, pl.ds(1, 15)], plane_ssem))
    for p, own, u, v in ((1, y, x, z), (0, x, y, z), (2, z, y, x)):
        total = ring_send[p, own].astype(F32)
        for d in range(3):
            wait_for(ring_recv.at[p, d], ring_rsem.at[p, d])
            total += ring_recv[p, d].astype(F32)
        plane_send[p] = total.astype(BF16)
        for du in FAR_FIRST:
            for dv in FAR_FIRST:
                if (du, dv) != (0, 0):
                    there = moved(*((0, du, dv), (du, 0, dv), (dv, du, 0))[p])
                    send(
                        plane_send.at[p, (u + du) % 4, (v + dv) % 4],
                        plane_recv.at[p, du * 4 + dv],
                        plane_ssem,
                        plane_rsem.at[p],
                        there,
                    )
        plane_recv[p, 0] = plane_send[p, u, v]

    for copy in late:
        copy.wait()
    send(schur.at[core], schur.at[core], schur_ssem, schur_rsem, partner)
    drains.append((schur.at[core], schur_ssem))
    for n in range(0, 3072, 768):
        right_ref[:256, n : n + 768] = base[n : n + 768].T
    first_t[...] = first[:, part(core * 128, 128)].T
    wait_for(schur.at[1 - core], schur_rsem)
    whole = schur[...].reshape(384, 384)
    high = whole.astype(BF16)
    split[0] = high
    split[1] = (whole - high.astype(F32)).astype(BF16)
    slot = x_lo * 4 + z
    for p in (1, 0, 2):
        lanes = slice(p * 128, p * 128 + 128)
        wait_for(plane_recv.at[p, pl.ds(1, 15)], plane_rsem.at[p])
        condensed[slot, :, lanes] = first_t[part(slot * 16, 16), lanes] - jnp.sum(plane_recv[p].astype(F32), axis=0)
    drains.append((condensed.at[pl.ds(0, 7)], gather_ssem))
    for dx in (1, 0):
        for dz in FAR_FIRST:
            if (dx, dz) != (0, 0):
                there = device(x_hi * 2 + (x_lo + dx) % 2, y, (z + dz) % 4, core)
                send(condensed.at[slot], condensed.at[slot], gather_ssem, gather_rsem, there)
    inverse_t[0] = inverse[0].T
    inverse_t[1] = inverse[1].T
    wait_for(condensed.at[pl.ds(0, 7)], gather_rsem)

    rows = condensed[...].reshape(128, 384)
    high = rows.astype(BF16)
    low = (rows - high.astype(F32)).astype(BF16)
    result = lax.dot_general(high, split[0], NT, preferred_element_type=F32)
    result += lax.dot_general(high, split[1], NT, preferred_element_type=F32)
    result += lax.dot_general(low, split[0], NT, preferred_element_type=F32)
    product[...] = result.astype(BF16).reshape(8, 16, 384)
    drains.append((product_recv, product_ssem))
    for dx in (1, 0):
        for dy in FAR_FIRST:
            if (dx, dy) != (0, 0):
                there_y, there_x = (y + dy) % 4, (x_hi + dx) % 2
                send(
                    product.at[there_y * 2 + there_x],
                    product_recv.at[dy * 2 + dx - 1],
                    product_ssem,
                    product_rsem,
                    device(there_x * 2 + x_lo, there_y, z, core),
                )
    for s in range(2):
        left_ref[s, :, 256:] = -primal[s]
    total = product[block].astype(F32)
    wait_for(product_recv, product_rsem)
    for k in range(7):
        total += product_recv[k].astype(F32)

    def spot(x, y, z):
        return adjoint.at[part(core * 128 + (y * 2 + x // 2) * 16, 16), part((z * 2 + x % 2) * 384, 384)]

    mine = spot(x, y, z)
    mine[...] = total.astype(BF16)
    spread = [(dx, dy, dz) for dz in FAR_FIRST for dx in FAR_FIRST for dy in FAR_FIRST][:63]
    for n, (dx, dy, dz) in enumerate(spread):
        there = device((x + dx) % 4, (y + dy) % 4, (z + dz) % 4, core)
        send(mine, mine, spread_ssem.at[n], spread_rsem.at[n], there)
        drains.append((mine, spread_ssem.at[n]))

    outs = []
    for group in range(4):
        lanes = part(((z - FAR_FIRST[group]) % 4) * 768, 768)
        outs.append(pltpu.make_async_copy(adjoint.at[:, lanes], right_ref.at[pl.ds(256, 256), lanes], out_sem.at[group]))

    def take(group):
        lanes = part(((z - FAR_FIRST[group]) % 4) * 768, 768)
        theirs = adjoint.at[part((1 - core) * 128, 128), lanes]
        wait_for(theirs, forward_rsem.at[group])
        outs[group].start()
        for s in range(2):
            term = lax.dot_general(coupling[s, :, lanes], adjoint[:, lanes], NT, preferred_element_type=F32)
            if group == 0:
                taken[s] = term
            else:
                taken[s] += term

    for group in range(4):
        for n in range(group * 16, min(group * 16 + 16, 63)):
            dx, dy, dz = spread[n]
            got = spot((x - dx) % 4, (y - dy) % 4, (z - dz) % 4)
            wait_for(got, spread_rsem.at[n])
        here = adjoint.at[part(core * 128, 128), part(((z - FAR_FIRST[group]) % 4) * 768, 768)]
        send(here, here, forward_ssem, forward_rsem.at[group], partner)
        if group:
            take(group - 1)
    drains.append((adjoint.at[part(core * 128, 128)], forward_ssem))
    wait_for(adjoint.at[part((1 - core) * 128, 128), part(z * 768, 768)], forward_rsem.at[3])
    outs[3].start()
    lanes = part(z * 768, 768)
    for s in range(2):
        term = lax.dot_general(coupling[s, :, lanes], adjoint[:, lanes], NT, preferred_element_type=F32)
        q = (cot[s].astype(F32) - (taken[s] + term)).astype(BF16)
        value = jnp.dot(inverse_t[s], q, preferred_element_type=F32)
        scen_ref[s] = value
        left_ref[s, :, :256] = -value.astype(BF16)
    for copy in outs:
        copy.wait()
    finish()


ROWS, SLOTS = 128, 4


def gradients(left, right, scen, columns, scen_hbm, first_ref, grad_hbm, buffer, scen_sem, sems):
    scen_copy = pltpu.make_async_copy(scen, scen_hbm, scen_sem)
    scen_copy.start()

    def write(n):
        rows = pl.ds(n * ROWS % 512, ROWS)
        return pltpu.make_async_copy(buffer.at[n % SLOTS], grad_hbm.at[n * ROWS // 512, rows], sems.at[n % SLOTS])

    steps = 1024 // ROWS
    for n in range(steps):
        if n >= SLOTS:
            write(n - SLOTS).wait()
        rows = pl.ds(n * ROWS % 512, ROWS)
        buffer[n % SLOTS] = jnp.dot(left[n * ROWS // 512, rows], right[...], preferred_element_type=F32)
        write(n).start()
    first_ref[...] = columns[...].astype(F32).T
    for n in range(steps - SLOTS, steps):
        write(n).wait()
    scen_copy.wait()


def body(scen_inverse, coupling, scen_cot, first_cot, schur_inverse, scen_primal, first_primal):
    any_space, vmem = pl.BlockSpec(memory_space=pl.ANY), pl.BlockSpec(memory_space=pltpu.VMEM)
    dma = pltpu.SemaphoreType.DMA
    operands = (scen_inverse, coupling, scen_cot, first_cot, schur_inverse.T, scen_primal, first_primal)
    scen, left, right = pl.pallas_call(
        exchange,
        out_shape=(
            jax.ShapeDtypeStruct((2, 512, 256), F32),
            jax.ShapeDtypeStruct((2, 512, 512), BF16),
            jax.ShapeDtypeStruct((512, 3072), BF16),
        ),
        in_specs=[any_space] * 7,
        out_specs=(vmem, vmem, vmem),
        scratch_shapes=[
            pltpu.VMEM((2, 512, 512), BF16),
            pltpu.VMEM((2, 512, 512), BF16),
            pltpu.VMEM((2, 512, 3072), BF16),
            pltpu.VMEM((2, 512, 256), BF16),
            pltpu.VMEM((2, 512, 256), BF16),
            pltpu.VMEM((3072, 256), BF16),
            pltpu.VMEM((384, 256), F32),
            pltpu.VMEM((2, 192, 384), F32),
            pltpu.VMEM((128, 384), F32),
            pltpu.VMEM((256, 1024), BF16),
            pltpu.VMEM((2, 384, 384), BF16),
            pltpu.VMEM((4, 128, 768), BF16),
            pltpu.VMEM((4, 128, 768), F32),
            pltpu.VMEM((4, 128, 768), BF16),
            pltpu.VMEM((3, 4, 4, 4, 16, 128), BF16),
            pltpu.VMEM((3, 3, 4, 4, 16, 128), BF16),
            pltpu.VMEM((3, 4, 4, 16, 128), BF16),
            pltpu.VMEM((3, 16, 16, 128), BF16),
            pltpu.VMEM((8, 16, 384), F32),
            pltpu.VMEM((8, 16, 384), BF16),
            pltpu.VMEM((7, 16, 384), BF16),
            pltpu.VMEM((256, 3072), BF16),
            pltpu.VMEM((2, 512, 256), F32),
            dma((6,)), dma((4,)), dma, dma((4,)), dma, dma,
            pltpu.SemaphoreType.REGULAR, dma((3,)), dma((3, 3)), dma, dma((3,)),
            dma, dma, dma, dma,
            dma((63,)), dma((63,)), dma, dma((4,)), dma((4,)),
        ],
        compiler_params=pltpu.CompilerParams(
            collective_id=0, has_side_effects=True, vmem_limit_bytes=36 * 1024 * 1024
        ),
        name="exchange",
    )(*(pltpu.with_memory_space_constraint(array, pltpu.HBM) for array in operands))
    columns = lax.dynamic_slice(right, (256, lax.axis_index("col") * 192), (256, 192))
    return pl.pallas_call(
        gradients,
        out_shape=(
            jax.ShapeDtypeStruct((2, 512, 256), F32),
            jax.ShapeDtypeStruct((192, 256), F32),
            jax.ShapeDtypeStruct((2, 512, 3072), F32),
        ),
        in_specs=[vmem] * 4,
        out_specs=(any_space, vmem, any_space),
        scratch_shapes=[pltpu.VMEM((SLOTS, ROWS, 3072), F32), dma, dma((SLOTS,))],
        compiler_params=pltpu.CompilerParams(vmem_limit_bytes=24 * 1024 * 1024),
        name="gradients",
    )(left, right, scen, columns)


def solution(mesh):
    return jax.shard_map(
        body,
        mesh=mesh,
        in_specs=(
            P(("row", "col"), None, None),
            P(("row", "col"), None, None),
            P(("row", "col"), None, None),
            P("row", None),
            P("row", "col"),
            P(("row", "col"), None, None),
            P(),
        ),
        out_specs=(P(("row", "col"), None, None), P("col", None), P(("row", "col"), None, None)),
        check_vma=False,
    )
```

```python
import functools

import jax
import jax.numpy as jnp
from jax import lax
from jax.experimental import pallas as pl
from jax.experimental.pallas import tpu as pltpu
from jax.sharding import PartitionSpec as P

MESH = pl.DeviceIdType.MESH
F32, BF16 = jnp.float32, jnp.bfloat16
FAR_FIRST = (2, 1, 3, 0)
NT = (((1,), (1,)), ((), ()))
TN = (((0,), (0,)), ((), ()))


def place():
    row, col = lax.axis_index("row"), lax.axis_index("col")
    return (row % 2) * 2 + (col // 2) % 2, row // 2, col // 4, col % 2


def device(x, y, z, core):
    return (y * 2 + x // 2, z * 4 + (x % 2) * 2 + core)


def part(start, size):
    return pl.ds(pl.multiple_of(start, size), size)


def wait_for(ref, sem):
    pltpu.make_async_copy(ref, ref, sem).wait()


def exchange(
    inverse_hbm, coupling_hbm, cot_hbm, first_hbm, schur_hbm, primal_hbm, base_hbm,
    scen_ref, left_ref, right_ref,
    inverse, inverse_t, coupling, cot, primal, base, first, schur, first_t, h_t, split,
    pair_send, pair_own, pair_recv, ring_send, ring_recv, plane_send, plane_recv,
    condensed, product, product_recv, adjoint, taken,
    load_sem, chunk_sem, pair_ssem, pair_rsem, schur_ssem, schur_rsem,
    near_sem, ring_ssem, ring_rsem, plane_ssem, plane_rsem,
    gather_ssem, gather_rsem, product_ssem, product_rsem,
    spread_ssem, spread_rsem, forward_ssem, forward_rsem, out_sem,
):
    x, y, z, core = place()
    x_hi, x_lo = x // 2, x % 2
    block, tile = y * 2 + x_hi, z * 2 + x_lo
    partner = device(x, y, z, 1 - core)
    drains = []

    def finish():
        for ref, sem in drains:
            wait_for(ref, sem)

    def send(source, target, ssem, rsem, to):
        copy = pltpu.make_async_remote_copy(
            src_ref=source, dst_ref=target, send_sem=ssem, recv_sem=rsem, device_id=to, device_id_type=MESH
        )
        copy.start()

    loads = []
    for s in range(2):
        loads.append(pltpu.make_async_copy(cot_hbm.at[s], cot.at[s], load_sem.at[2 * s]))
        loads.append(pltpu.make_async_copy(inverse_hbm.at[s], inverse.at[s], load_sem.at[2 * s + 1]))
    for copy in loads:
        copy.start()
    chunks = []
    for k, dy in enumerate(FAR_FIRST):
        lanes = part(((y + dy) % 4) * 768, 768)
        chunks.append(
            pltpu.make_async_copy(coupling_hbm.at[:, :, lanes], coupling.at[:, :, lanes], chunk_sem.at[k])
        )
    chunks[0].start()
    chunks[1].start()

    here = (x, y, z)

    def moved(*steps):
        spot = [(c + d) % 4 for c, d in zip(here, steps)]
        return device(*spot, core)

    barrier = pltpu.get_barrier_semaphore()
    x_ring = [moved(d, 0, 0) for d in (1, 2, 3)]
    y_ring = [moved(0, d, 0) for d in (1, 2, 3)]
    z_ring = [moved(0, 0, d) for d in (1, 2, 3)]
    for there in x_ring + y_ring + z_ring + [partner]:
        pl.semaphore_signal(barrier, inc=1, device_id=there, device_id_type=MESH)

    late = [
        pltpu.make_async_copy(first_hbm, first, load_sem.at[4]),
        pltpu.make_async_copy(schur_hbm, schur.at[core], load_sem.at[5]),
        pltpu.make_async_copy(primal_hbm, primal, load_sem.at[6]),
        pltpu.make_async_copy(base_hbm, base, load_sem.at[7]),
    ]
    for s in range(2):
        loads[2 * s].wait()
        loads[2 * s + 1].wait()
        chunks[2 + s].start()
        helper = lax.dot_general(cot[s], inverse[s], TN, preferred_element_type=F32).astype(BF16)
        h_t[part((1 - core) * 128, 128), s * 512 : (s + 1) * 512] = helper[:128]
        h_t[part(core * 128, 128), s * 512 : (s + 1) * 512] = helper[128:]

    def local_sum(k):
        lanes = part(((y + FAR_FIRST[k]) % 4) * 768, 768)
        chunks[k].wait()
        if k == 3:
            for copy in late:
                copy.start()
        total = jnp.dot(h_t[...], coupling[:, :, lanes].reshape(1024, 768), preferred_element_type=F32)
        pair_send[k] = total[:128].astype(BF16)
        pair_own[k] = total[128:]

    def to_pair(k):
        send(pair_send.at[k], pair_recv.at[k], pair_ssem, pair_rsem.at[k], partner)

    def to_rings(k):
        wait_for(pair_recv.at[k], pair_rsem.at[k])
        there_y = (y + FAR_FIRST[k]) % 4
        total = (pair_own[k] + pair_recv[k].astype(F32)).astype(BF16)
        for hi in range(2):
            for lo in range(2):
                column = hi * 2 + lo
                for p in range(3):
                    lane = hi * 384 + p * 128
                    tiles = total[lo * 64 : lo * 64 + 64, lane : lane + 128].reshape(4, 16, 128)
                    if p == 0:
                        ring_send[0, column, there_y] = tiles
                    elif p == 1:
                        ring_send[1, there_y, column] = tiles
                    else:
                        ring_send[2, :, there_y, column] = tiles
        for d in (2, 1, 3):
            for p, own in ((0, x), (2, z)):
                send(
                    ring_send.at[p, (own + d) % 4, there_y],
                    ring_recv.at[p, d - 1, there_y],
                    ring_ssem.at[p],
                    ring_rsem.at[p, d - 1],
                    (x_ring if p == 0 else z_ring)[d - 1],
                )
        d = FAR_FIRST[k]
        if d:
            send(ring_send.at[1, there_y], ring_recv.at[1, d - 1], ring_ssem.at[1], ring_rsem.at[1, d - 1], y_ring[d - 1])

    drains.append((pair_send, pair_ssem))
    for p in range(3):
        drains.append((ring_recv.at[p], ring_ssem.at[p]))
    local_sum(0)
    pl.semaphore_wait(barrier, 10)
    to_pair(0)
    for there in x_ring + y_ring:
        pl.semaphore_signal(near_sem, inc=1, device_id=there, device_id_type=MESH)
    local_sum(1)
    to_pair(1)
    to_rings(0)
    local_sum(2)
    to_pair(2)
    to_rings(1)
    local_sum(3)
    to_pair(3)
    to_rings(2)
    to_rings(3)

    pl.semaphore_wait(near_sem, 6)
    drains.append((plane_recv.at[:, pl.ds(1, 15)], plane_ssem))
    for p, own, u, v in ((1, y, x, z), (0, x, y, z), (2, z, y, x)):
        total = ring_send[p, own].astype(F32)
        for d in range(3):
            wait_for(ring_recv.at[p, d], ring_rsem.at[p, d])
            total += ring_recv[p, d].astype(F32)
        plane_send[p] = total.astype(BF16)
        for du in FAR_FIRST:
            for dv in FAR_FIRST:
                if (du, dv) != (0, 0):
                    there = moved(*((0, du, dv), (du, 0, dv), (dv, du, 0))[p])
                    send(
                        plane_send.at[p, (u + du) % 4, (v + dv) % 4],
                        plane_recv.at[p, du * 4 + dv],
                        plane_ssem,
                        plane_rsem.at[p],
                        there,
                    )
        plane_recv[p, 0] = plane_send[p, u, v]

    for copy in late:
        copy.wait()
    send(schur.at[core], schur.at[core], schur_ssem, schur_rsem, partner)
    drains.append((schur.at[core], schur_ssem))
    for n in range(0, 3072, 768):
        right_ref[:256, n : n + 768] = base[n : n + 768].T
    first_t[...] = first[:, part(core * 128, 128)].T
    wait_for(schur.at[1 - core], schur_rsem)
    whole = schur[...].reshape(384, 384)
    high = whole.astype(BF16)
    split[0] = high
    split[1] = (whole - high.astype(F32)).astype(BF16)
    slot = x_lo * 4 + z
    for p in (1, 0, 2):
        lanes = slice(p * 128, p * 128 + 128)
        wait_for(plane_recv.at[p, pl.ds(1, 15)], plane_rsem.at[p])
        condensed[slot, :, lanes] = first_t[part(slot * 16, 16), lanes] - jnp.sum(plane_recv[p].astype(F32), axis=0)
    drains.append((condensed.at[pl.ds(0, 7)], gather_ssem))
    for dx in (1, 0):
        for dz in FAR_FIRST:
            if (dx, dz) != (0, 0):
                there = device(x_hi * 2 + (x_lo + dx) % 2, y, (z + dz) % 4, core)
                send(condensed.at[slot], condensed.at[slot], gather_ssem, gather_rsem, there)
    inverse_t[0] = inverse[0].T
    inverse_t[1] = inverse[1].T
    wait_for(condensed.at[pl.ds(0, 7)], gather_rsem)

    rows = condensed[...].reshape(128, 384)
    high = rows.astype(BF16)
    low = (rows - high.astype(F32)).astype(BF16)
    result = lax.dot_general(high, split[0], NT, preferred_element_type=F32)
    result += lax.dot_general(high, split[1], NT, preferred_element_type=F32)
    result += lax.dot_general(low, split[0], NT, preferred_element_type=F32)
    product[...] = result.astype(BF16).reshape(8, 16, 384)
    drains.append((product_recv, product_ssem))
    for dx in (1, 0):
        for dy in FAR_FIRST:
            if (dx, dy) != (0, 0):
                there_y, there_x = (y + dy) % 4, (x_hi + dx) % 2
                send(
                    product.at[there_y * 2 + there_x],
                    product_recv.at[dy * 2 + dx - 1],
                    product_ssem,
                    product_rsem,
                    device(there_x * 2 + x_lo, there_y, z, core),
                )
    for s in range(2):
        left_ref[s, :, 256:] = -primal[s]
    total = product[block].astype(F32)
    wait_for(product_recv, product_rsem)
    for k in range(7):
        total += product_recv[k].astype(F32)

    def spot(x, y, z):
        return adjoint.at[part(core * 128 + (y * 2 + x // 2) * 16, 16), part((z * 2 + x % 2) * 384, 384)]

    mine = spot(x, y, z)
    mine[...] = total.astype(BF16)
    spread = [(dx, dy, dz) for dz in FAR_FIRST for dx in FAR_FIRST for dy in FAR_FIRST][:63]
    for n, (dx, dy, dz) in enumerate(spread):
        there = device((x + dx) % 4, (y + dy) % 4, (z + dz) % 4, core)
        send(mine, mine, spread_ssem.at[n], spread_rsem.at[n], there)
        drains.append((mine, spread_ssem.at[n]))

    outs = []
    for group in range(4):
        lanes = part(((z - FAR_FIRST[group]) % 4) * 768, 768)
        outs.append(pltpu.make_async_copy(adjoint.at[:, lanes], right_ref.at[pl.ds(256, 256), lanes], out_sem.at[group]))

    def take(group):
        lanes = part(((z - FAR_FIRST[group]) % 4) * 768, 768)
        theirs = adjoint.at[part((1 - core) * 128, 128), lanes]
        wait_for(theirs, forward_rsem.at[group])
        outs[group].start()
        for s in range(2):
            term = lax.dot_general(coupling[s, :, lanes], adjoint[:, lanes], NT, preferred_element_type=F32)
            if group == 0:
                taken[s] = term
            else:
                taken[s] += term

    for group in range(4):
        for n in range(group * 16, min(group * 16 + 16, 63)):
            dx, dy, dz = spread[n]
            got = spot((x - dx) % 4, (y - dy) % 4, (z - dz) % 4)
            wait_for(got, spread_rsem.at[n])
        here = adjoint.at[part(core * 128, 128), part(((z - FAR_FIRST[group]) % 4) * 768, 768)]
        send(here, here, forward_ssem, forward_rsem.at[group], partner)
        if group:
            take(group - 1)
    drains.append((adjoint.at[part(core * 128, 128)], forward_ssem))
    wait_for(adjoint.at[part((1 - core) * 128, 128), part(z * 768, 768)], forward_rsem.at[3])
    outs[3].start()
    lanes = part(z * 768, 768)
    for s in range(2):
        term = lax.dot_general(coupling[s, :, lanes], adjoint[:, lanes], NT, preferred_element_type=F32)
        q = (cot[s].astype(F32) - (taken[s] + term)).astype(BF16)
        value = jnp.dot(inverse_t[s], q, preferred_element_type=F32)
        scen_ref[s] = value
        left_ref[s, :, :256] = -value.astype(BF16)
    for copy in outs:
        copy.wait()
    finish()


ROWS, SLOTS = 128, 4


def gradients(left, right, scen, scen_hbm, first_ref, grad_hbm, buffer, tile, scen_sem, sems):
    scen_copy = pltpu.make_async_copy(scen, scen_hbm, scen_sem)
    scen_copy.start()

    def write(n):
        rows = pl.ds(n * ROWS % 512, ROWS)
        return pltpu.make_async_copy(buffer.at[n % SLOTS], grad_hbm.at[n * ROWS // 512, rows], sems.at[n % SLOTS])

    steps = 1024 // ROWS
    for n in range(steps):
        if n >= SLOTS:
            write(n - SLOTS).wait()
        rows = pl.ds(n * ROWS % 512, ROWS)
        buffer[n % SLOTS] = jnp.dot(left[n * ROWS // 512, rows], right[...], preferred_element_type=F32)
        write(n).start()
    column = lax.axis_index("col")
    tile[...] = right[256:, part(column // 2 * 384, 384)].astype(F32).T
    first_ref[...] = tile[part(column % 2 * 192, 192)]
    for n in range(steps - SLOTS, steps):
        write(n).wait()
    scen_copy.wait()


def body(scen_inverse, coupling, scen_cot, first_cot, schur_inverse, scen_primal, first_primal):
    any_space, vmem = pl.BlockSpec(memory_space=pl.ANY), pl.BlockSpec(memory_space=pltpu.VMEM)
    dma = pltpu.SemaphoreType.DMA
    operands = (scen_inverse, coupling, scen_cot, first_cot, schur_inverse.T, scen_primal, first_primal)
    scen, left, right = pl.pallas_call(
        exchange,
        out_shape=(
            jax.ShapeDtypeStruct((2, 512, 256), F32),
            jax.ShapeDtypeStruct((2, 512, 512), BF16),
            jax.ShapeDtypeStruct((512, 3072), BF16),
        ),
        in_specs=[any_space] * 7,
        out_specs=(vmem, vmem, vmem),
        scratch_shapes=[
            pltpu.VMEM((2, 512, 512), BF16),
            pltpu.VMEM((2, 512, 512), BF16),
            pltpu.VMEM((2, 512, 3072), BF16),
            pltpu.VMEM((2, 512, 256), BF16),
            pltpu.VMEM((2, 512, 256), BF16),
            pltpu.VMEM((3072, 256), BF16),
            pltpu.VMEM((384, 256), F32),
            pltpu.VMEM((2, 192, 384), F32),
            pltpu.VMEM((128, 384), F32),
            pltpu.VMEM((256, 1024), BF16),
            pltpu.VMEM((2, 384, 384), BF16),
            pltpu.VMEM((4, 128, 768), BF16),
            pltpu.VMEM((4, 128, 768), F32),
            pltpu.VMEM((4, 128, 768), BF16),
            pltpu.VMEM((3, 4, 4, 4, 16, 128), BF16),
            pltpu.VMEM((3, 3, 4, 4, 16, 128), BF16),
            pltpu.VMEM((3, 4, 4, 16, 128), BF16),
            pltpu.VMEM((3, 16, 16, 128), BF16),
            pltpu.VMEM((8, 16, 384), F32),
            pltpu.VMEM((8, 16, 384), BF16),
            pltpu.VMEM((7, 16, 384), BF16),
            pltpu.VMEM((256, 3072), BF16),
            pltpu.VMEM((2, 512, 256), F32),
            dma((8,)), dma((4,)), dma, dma((4,)), dma, dma,
            pltpu.SemaphoreType.REGULAR, dma((3,)), dma((3, 3)), dma, dma((3,)),
            dma, dma, dma, dma,
            dma((63,)), dma((63,)), dma, dma((4,)), dma((4,)),
        ],
        compiler_params=pltpu.CompilerParams(
            collective_id=0, has_side_effects=True, vmem_limit_bytes=36 * 1024 * 1024
        ),
        name="exchange",
    )(*(pltpu.with_memory_space_constraint(array, pltpu.HBM) for array in operands))
    return pl.pallas_call(
        gradients,
        out_shape=(
            jax.ShapeDtypeStruct((2, 512, 256), F32),
            jax.ShapeDtypeStruct((192, 256), F32),
            jax.ShapeDtypeStruct((2, 512, 3072), F32),
        ),
        in_specs=[vmem] * 3,
        out_specs=(any_space, vmem, any_space),
        scratch_shapes=[pltpu.VMEM((SLOTS, ROWS, 3072), F32), pltpu.VMEM((384, 256), F32), dma, dma((SLOTS,))],
        compiler_params=pltpu.CompilerParams(vmem_limit_bytes=24 * 1024 * 1024),
        name="gradients",
    )(left, right, scen)


def solution(mesh):
    return jax.shard_map(
        body,
        mesh=mesh,
        in_specs=(
            P(("row", "col"), None, None),
            P(("row", "col"), None, None),
            P(("row", "col"), None, None),
            P("row", None),
            P("row", "col"),
            P(("row", "col"), None, None),
            P(),
        ),
        out_specs=(P(("row", "col"), None, None), P("col", None), P(("row", "col"), None, None)),
        check_vma=False,
    )
```
